512 devices in a mesh: seq: 16 (over y, x), dp: 32 (over z, core).
Axes of the slice: x: 4, y: 4, z: 16, core: 2. Of those that a mesh axis runs over, the one named last changes fastest.
Arguments:
- queries: bfloat16 [32, 2048, 2048], P('dp', 'seq'), may hold values from -30 to 30
- key_states: bfloat16 [32, 2048, 2048], P('dp', 'seq'), may hold values from -4.5 to 4.5
- value_states: bfloat16 [32, 2048, 2048], P('dp', 'seq'), may hold values from -6 to 6
- grad_out: bfloat16 [32, 2048, 2048], P('dp', 'seq'), may hold values from -18 to 18
- out_weight: bfloat16 [2048, 2048], P('dp'), may hold values from -0.125 to 0.125
- block_lists: int32 [16, 16, 8], P('seq'), may hold values from 0 to 15, as said below
- block_counts: int32 [16, 16], P('seq'), may hold values from 1 to 8, as said below
Outputs:
- query_grad: bfloat16 [32, 2048, 2048], P('dp', 'seq')
- key_grad: bfloat16 [32, 2048, 2048], P('dp', 'seq')
- value_grad: bfloat16 [32, 2048, 2048], P('dp', 'seq')
The draws below stay inside these ranges and needn't reach their ends.
Inputs may be any that keep to these rules, and one draw needn't show every extreme that they name: The entries of one row block_lists[h, i, :] are distinct. `block_counts`: the counts of one head sum to at most 64; in every draw some head sums to exactly 64 and some query block uses all 8 entries.
All inputs are finite; a program needn't handle non-finite values.
Results may differ from the reference program's by a relative error of at most 0.0093.
Values may be sent and summed in bfloat16 or wider, within the bound.
A program may use at most 64 MiB of HBM per device.

```python
import jax
import jax.numpy as jnp
from jax import lax

D = 2048
H = 16
HD = 128
SEQ_LEN = 2048
SEQS = 32
NB = 16
KMAX = 8


def field_pair(key):
    base_key = jax.random.fold_in(key, 17)
    query_key, other_key = jax.random.split(base_key, 2)
    field_shape = (SEQS, SEQ_LEN, D)
    query_field = jnp.clip(jax.random.normal(query_key, field_shape, jnp.float32), -4.5, 4.5)
    key_field = jnp.clip(jax.random.normal(other_key, field_shape, jnp.float32), -4.5, 4.5)
    return (query_field, key_field)


def draw_queries(key, part):
    return field_pair(key)[0].astype(jnp.bfloat16)


def draw_key_states(key, part):
    return field_pair(key)[1].astype(jnp.bfloat16)


def pattern_pair(key):
    base_key = jax.random.fold_in(key, 29)
    perm_key, light_key, busy_key, spike_key, split_key, peak_key, order_key = jax.random.split(base_key, 7)
    extra_offsets = jax.vmap(lambda head_key: jax.random.permutation(head_key, NB - 3))(jax.random.split(perm_key, H))
    extra_offsets = extra_offsets.astype(jnp.int32) + 2
    window_offsets = jnp.broadcast_to(jnp.array([0, 1, NB - 1], jnp.int32), (H, 3))
    offsets = jnp.concatenate([window_offsets, extra_offsets], axis=1)[:, :KMAX]
    slot_order = jax.vmap(lambda head_key: jax.random.permutation(head_key, KMAX))(jax.random.split(order_key, H))
    offsets = jnp.take_along_axis(offsets, slot_order.astype(jnp.int32), axis=1)
    block_index = jnp.arange(NB, dtype=jnp.int32)
    block_table = (block_index[None, :, None] + offsets[:, None, :]) % NB
    light_counts = jax.random.randint(light_key, (H, NB), 1, max(2, KMAX // 2))
    busy_head = jax.random.randint(busy_key, (), 0, H)
    spike_head = (busy_head + 1 + jax.random.randint(spike_key, (), 0, H - 1)) % H
    first_half = jax.random.randint(split_key, (NB // 2,), 1, KMAX)
    heavy_counts = jnp.stack([first_half, KMAX - first_half], axis=1).reshape(NB)
    peak_block = jax.random.randint(peak_key, (), 0, NB)
    spike_counts = jnp.where(block_index == peak_block, KMAX, 1)
    head_index = jnp.arange(H, dtype=jnp.int32)[:, None]
    count_table = jnp.where(head_index == busy_head, heavy_counts[None, :], jnp.where(head_index == spike_head, spike_counts[None, :], light_counts))
    return (block_table.astype(jnp.int32), count_table.astype(jnp.int32))


def draw_block_lists(key, part):
    return pattern_pair(key)[0]


def draw_block_counts(key, part):
    return pattern_pair(key)[1]


def shard_levels(rng, extent, cuts, low, high):
    loudness = 1.0
    for dim, blocks in cuts:
        draws = jax.random.uniform(jax.random.fold_in(jax.random.fold_in(rng, 6), dim), (blocks,), jnp.float32, low / len(cuts), high / len(cuts))
        loudness = loudness * jnp.repeat(jnp.exp(draws), extent[dim] // blocks).reshape((-1,) + (1,) * (len(extent) - 1 - dim))
    return loudness


def centred(own_key, dims, spread, limit, pieces=(), kind=jnp.bfloat16):
    loudness = shard_levels(own_key, dims, pieces, -0.22, 0.18) if pieces else 1.0
    entries = jax.random.normal(own_key, dims, jnp.float32) * spread * loudness
    return jnp.minimum(jnp.maximum(entries, -limit), limit).astype(kind)


def setup_inputs(seed: int = 0) -> dict:
    streams_of = jax.random.split(jax.random.key(seed), 8)
    queries = draw_queries(jax.random.fold_in(streams_of[7], 71), 0)
    key_states = draw_key_states(jax.random.fold_in(streams_of[7], 71), 0)
    value_states = centred(streams_of[2], (SEQS, SEQ_LEN, D), 1.0, 6.0, ((0, 32), (1, 16)))
    grad_out = centred(streams_of[3], (SEQS, SEQ_LEN, D), 3.0, 18.0, ((0, 32), (1, 16)))
    out_weight = centred(streams_of[4], (D, D), D ** -0.5, 0.125, ((0, 32),))
    block_lists = draw_block_lists(jax.random.fold_in(streams_of[7], 71), 0)
    block_counts = draw_block_counts(jax.random.fold_in(streams_of[7], 71), 0)
    return dict(queries=queries, key_states=key_states, value_states=value_states, grad_out=grad_out, out_weight=out_weight, block_lists=block_lists, block_counts=block_counts)


def head_grads(operands):
    query_head, key_head, value_head, grad_head, lists_head, counts_head = operands
    nblocks, kslots = lists_head.shape
    head_width = query_head.shape[-1]
    score_scale = head_width ** -0.5
    query_blocks = query_head.reshape(nblocks, -1, head_width).astype(jnp.float32)
    key_blocks = key_head.reshape(nblocks, -1, head_width)
    value_blocks = value_head.reshape(nblocks, -1, head_width)
    grad_blocks = grad_head.reshape(nblocks, -1, head_width).astype(jnp.float32)
    key_sets = key_blocks[lists_head].astype(jnp.float32)
    value_sets = value_blocks[lists_head].astype(jnp.float32)
    live_slots = jnp.arange(kslots, dtype=jnp.int32)[None, :] < counts_head[:, None]
    scores = jnp.einsum('iqd,ijkd->iqjk', query_blocks, key_sets) * score_scale
    scores = jnp.where(live_slots[:, None, :, None], scores, -jnp.inf)
    row_top = jnp.max(scores, axis=(2, 3), keepdims=True)
    weights = jnp.exp(scores - row_top)
    attn_probs = weights / jnp.sum(weights, axis=(2, 3), keepdims=True)
    probs_low = lax.optimization_barrier(attn_probs.astype(jnp.bfloat16)).astype(jnp.float32)
    attn_out = jnp.einsum('iqjk,ijkd->iqd', probs_low, value_sets)
    row_delta = jnp.sum(grad_blocks * attn_out, axis=-1)
    prob_grad = jnp.einsum('iqd,ijkd->iqjk', grad_blocks, value_sets)
    score_grad = attn_probs * (prob_grad - row_delta[:, :, None, None])
    score_low = lax.optimization_barrier(score_grad.astype(jnp.bfloat16)).astype(jnp.float32)
    query_sum = jnp.einsum('iqjk,ijkd->iqd', score_low, key_sets) * score_scale
    key_parts = jnp.einsum('iqjk,iqd->ijkd', score_low, query_blocks)
    value_parts = jnp.einsum('iqjk,iqd->ijkd', probs_low, grad_blocks)
    empty_sum = jnp.zeros((nblocks, query_blocks.shape[1], head_width), jnp.float32)
    key_sum = empty_sum.at[lists_head].add(key_parts) * score_scale
    value_sum = empty_sum.at[lists_head].add(value_parts)
    return (query_sum.reshape(-1, head_width).astype(jnp.bfloat16),
            key_sum.reshape(-1, head_width).astype(jnp.bfloat16),
            value_sum.reshape(-1, head_width).astype(jnp.bfloat16))


def to_heads(matrix):
    return jnp.transpose(matrix.reshape(SEQ_LEN, H, HD), (1, 0, 2))


def from_heads(stacked):
    return jnp.transpose(stacked, (1, 0, 2)).reshape(SEQ_LEN, D)


def one_sequence(operands):
    query_rows, key_rows, value_rows, grad_rows, out_weight, block_lists, block_counts = operands
    attn_grad = jnp.dot(grad_rows, out_weight.T, preferred_element_type=jnp.float32).astype(jnp.bfloat16)
    query_heads, key_heads, value_heads = lax.map(
        head_grads,
        (to_heads(query_rows), to_heads(key_rows), to_heads(value_rows), to_heads(attn_grad), block_lists, block_counts))
    return (from_heads(query_heads), from_heads(key_heads), from_heads(value_heads))


def reference(queries, key_states, value_states, grad_out, out_weight, block_lists, block_counts):
    def per_sequence(rows_tuple):
        query_rows, key_rows, value_rows, grad_rows = rows_tuple
        return one_sequence((query_rows, key_rows, value_rows, grad_rows, out_weight, block_lists, block_counts))

    query_grad, key_grad, value_grad = lax.map(per_sequence, (queries, key_states, value_states, grad_out))
    return (query_grad, key_grad, value_grad)
```

```python
import functools

import jax
import jax.numpy as jnp
from jax import lax
from jax.experimental import pallas as pl
from jax.experimental.pallas import tpu as pltpu
from jax.sharding import PartitionSpec as P

MESH = pl.DeviceIdType.MESH
HD = 128
NS = 16
NZ = 16
NBLK = 16
TOK = 128
HALF = HD // 2
PIECES = 2
PROWS = HALF // 2 // PIECES
FWD, BWD = 0, 1
HOPS = (NZ // 2, NZ // 2 - 1)
OFFSETS = (
    (1, 0), (3, 0), (0, 1), (0, 3), (1, 1), (3, 3), (1, 3), (3, 1),
    (2, 0), (0, 2), (2, 1), (2, 3), (1, 2), (3, 2), (2, 2),
)


def aligned(index, size):
    return pl.ds(pl.multiple_of(index * size, size), size)


def plane_peers(seq):
    y, x = seq // 4, seq % 4
    return [((y + dy) % 4) * 4 + (x + dx) % 4 for dx, dy in OFFSETS]


def enter(devices):
    barrier = pltpu.get_barrier_semaphore()
    for device in devices:
        pl.semaphore_signal(barrier, inc=1, device_id=device, device_id_type=MESH)
    pl.semaphore_wait(barrier, len(devices))


def remote(src, dst, send_sem, recv_sem, device):
    return pltpu.make_async_remote_copy(
        src_ref=src, dst_ref=dst, send_sem=send_sem, recv_sem=recv_sem,
        device_id=device, device_id_type=MESH,
    )


def weight_rows(hop, way):
    if hop == 0:
        return 0, 0
    if hop == NZ // 2:
        return 0, HALF
    return hop, way * HALF


def gather_kernel(
    q_in, k_in, v_in, g_in, w_in, q_out, k_out, v_out, gt_out,
    rows, weights, product,
    head_send, head_recv, head_local, row_send, row_recv, row_local,
    w_local, w_send0, own_send, own_recv, w_send, w_recv, core_send, core_recv,
    g_send, g_recv, g_local,
):
    seq, dp = lax.axis_index("seq"), lax.axis_index("dp")
    z, core = dp // 2, dp % 2
    side = seq % 2
    pair = seq + 1 - 2 * side
    partner = (seq, z * 2 + 1 - core)
    peers = plane_peers(seq)

    def along(way, c):
        step = 1 if way == FWD else NZ - 1
        return (seq, ((z + step) % NZ) * 2 + c)

    enter(
        [(p, dp) for p in peers]
        + [partner]
        + [along(way, c) for way in (FWD, BWD) for c in (0, 1)]
    )

    def first_copies():
        copies = []
        for piece in range(PIECES):
            for way in (FWD, BWD):
                slot, base = weight_rows(1, way)
                for c in (0, 1):
                    at = c * (HALF // 2) + piece * PROWS
                    copies.append(remote(
                        w_in.at[pl.ds(at, PROWS), :],
                        weights.at[slot, pl.ds(base + at, PROWS), :],
                        w_send0.at[way, c, piece], w_recv.at[way, 1, piece],
                        along(way, c),
                    ))
        copies.append(remote(
            w_in, weights.at[0, pl.ds(0, HALF), :], own_send, own_recv, partner
        ))
        return copies

    own_copy = pltpu.make_async_copy(w_in, weights.at[0, pl.ds(0, HALF), :], w_local)

    @pl.when(core == side)
    def _():
        for copy in first_copies():
            copy.start()
        own_copy.start()

    row_copy = remote(
        g_in, rows.at[aligned(side, TOK), :], row_send, row_recv, (pair, dp)
    )
    row_copy.start()
    row_here = pltpu.make_async_copy(g_in, rows.at[aligned(side, TOK), :], row_local)
    row_here.start()

    head_copies, head_here = [], []
    for n, (src, dst) in enumerate(((q_in, q_out), (k_in, k_out), (v_in, v_out))):
        copy = pltpu.make_async_copy(
            src.at[:, aligned(seq, HD)], dst.at[aligned(seq, TOK), :], head_local.at[n]
        )
        copy.start()
        head_here.append(copy)
        for m, p in enumerate(peers):
            copy = remote(
                src.at[:, aligned(p, HD)], dst.at[aligned(seq, TOK), :],
                head_send.at[n, m], head_recv.at[n, m], (p, dp),
            )
            copy.start()
            head_copies.append(copy)

    def quarter(hop, way, c, piece):
        slot, base = weight_rows(hop, way)
        at = base + piece * PROWS + c * (HALF // 2)
        return weights.at[slot, pl.ds(pl.multiple_of(at, PROWS), PROWS), :]

    def onward(hop, way, piece):
        return remote(
            quarter(hop, way, core, piece), quarter(hop + 1, way, core, piece),
            w_send.at[way, hop, piece], w_recv.at[way, hop + 1, piece],
            along(way, core),
        )

    def arrival(hop, way, piece):
        here = quarter(hop, way, core, piece)
        return remote(
            here, here, w_send.at[way, hop, piece], w_recv.at[way, hop, piece],
            along(way, core),
        )

    def across(hop, way, piece):
        here = quarter(hop, way, core, piece)
        return remote(
            here, here, core_send.at[way, hop, piece], core_recv.at[way, hop, piece],
            partner,
        )

    def head_send_copy(slot, way, owner):
        return remote(
            product.at[slot, pl.ds(way * HALF, HALF), :],
            gt_out.at[aligned(side, HALF), aligned(seq // 2, 2 * TOK)],
            g_send.at[slot, way], g_recv.at[seq], (owner, dp),
        )

    def head_local_copy(slot, way):
        return pltpu.make_async_copy(
            product.at[slot, pl.ds(way * HALF, HALF), :],
            gt_out.at[aligned(side, HALF), aligned(seq // 2, 2 * TOK)],
            g_local,
        )

    def owners(slot):
        if slot == 0:
            return z, (z + NZ // 2) % NZ
        return (z + NZ - slot) % NZ, (z + slot) % NZ

    def project(slot):
        product[slot] = lax.dot_general(
            weights[slot], rows[...], (((1,), (1,)), ((), ())),
            preferred_element_type=jnp.float32,
        ).astype(jnp.bfloat16)
        for way, owner in enumerate(owners(slot)):
            @pl.when(owner != seq)
            def _(way=way, owner=owner):
                head_send_copy(slot, way, owner).start()

            @pl.when(owner == seq)
            def _(way=way):
                head_local_copy(slot, way).start()

    for hop in range(1, NZ // 2 + 1):
        ways = [way for way in (FWD, BWD) if hop <= HOPS[way]]
        for piece in range(PIECES):
            for way in ways:
                arrival(hop, way, piece).wait_recv()
                if hop < HOPS[way]:
                    onward(hop, way, piece).start()
                across(hop, way, piece).start()
        if hop == 1:
            row_here.wait()
            row_copy.wait()
        else:
            for piece in range(PIECES):
                for way in (FWD, BWD):
                    across(hop - 1, way, piece).wait_recv()
            project(hop - 1)
    for piece in range(PIECES):
        across(NZ // 2, FWD, piece).wait_recv()

    @pl.when(core == side)
    def _():
        own_copy.wait()

    @pl.when(core != side)
    def _():
        remote(
            w_in, weights.at[0, pl.ds(0, HALF), :], own_send, own_recv, partner
        ).wait_recv()

    project(0)

    @pl.when(core == side)
    def _():
        for copy in first_copies():
            copy.wait_send()

    for hop in range(1, NZ // 2 + 1):
        for piece in range(PIECES):
            for way in (FWD, BWD):
                if hop < HOPS[way]:
                    onward(hop, way, piece).wait_send()
                if hop <= HOPS[way]:
                    across(hop, way, piece).wait_send()
    for copy in head_here:
        copy.wait()
    for copy in head_copies:
        copy.wait()
    for slot in range(NZ // 2):
        for way, owner in enumerate(owners(slot)):
            @pl.when(owner != seq)
            def _(slot=slot, way=way, owner=owner):
                head_send_copy(slot, way, owner).wait_send()

            @pl.when(owner == seq)
            def _(slot=slot, way=way):
                head_local_copy(slot, way).wait()
    for other in range(NS):
        @pl.when(other != seq)
        def _(other=other):
            block = gt_out.at[pl.ds(0, HALF), pl.ds(0, 2 * TOK)]
            remote(
                block, block, g_send.at[0, 0], g_recv.at[other], (other, dp)
            ).wait_recv()


def gather_heads(q, k, v, g, w):
    dma = pltpu.SemaphoreType.DMA
    heads = jax.ShapeDtypeStruct((NS * TOK, HD), jnp.bfloat16)
    turned = jax.ShapeDtypeStruct((HD, NS * TOK), jnp.bfloat16)
    width = g.shape[1]
    anywhere = pl.BlockSpec(memory_space=pl.ANY)
    hops = NZ // 2 + 1
    return pl.pallas_call(
        gather_kernel,
        name="gather_heads",
        out_shape=[heads, heads, heads, turned],
        in_specs=[anywhere] * 5,
        out_specs=[anywhere] * 4,
        scratch_shapes=[
            pltpu.VMEM((2 * TOK, width), jnp.bfloat16),
            pltpu.VMEM((NZ // 2, HD, width), jnp.bfloat16),
            pltpu.VMEM((NZ // 2, HD, 2 * TOK), jnp.bfloat16),
            dma((3, len(OFFSETS))), dma((3, len(OFFSETS))), dma((3,)),
            dma, dma, dma,
            dma, dma((2, 2, PIECES)), dma, dma,
            dma((2, hops, PIECES)), dma((2, hops, PIECES)),
            dma((2, hops, PIECES)), dma((2, hops, PIECES)),
            dma((NZ // 2, 2)), dma((NS,)), dma,
        ],
        compiler_params=pltpu.CompilerParams(
            collective_id=0, has_side_effects=True, vmem_limit_bytes=24 << 20
        ),
    )(q, k, v, g, w)


def attention_kernel(
    lists, counts, q, k, v, gt, dq, dk, dv, k_turned, score, prob_grad, dk_sum, dv_sum
):
    scale = HD ** -0.5
    exponent = scale * 1.4426950408889634
    dk_sum[...] = jnp.zeros_like(dk_sum)
    dv_sum[...] = jnp.zeros_like(dv_sum)
    for t in range(NBLK):
        k_turned[t] = k[pl.ds(t * TOK, TOK), :].T

    def fold(x, op):
        return op(x.reshape(TOK // 8, 8, TOK), axis=0)

    def query_block(i, carry):
        q_rows = q[aligned(i, TOK), :]
        g_cols = gt[:, aligned(i, TOK)]
        g_rows = g_cols.T

        def run(n):
            blocks = [lists[0, i, j] for j in range(n)]
            top = None
            for j, t in enumerate(blocks):
                s = lax.dot_general(
                    k[aligned(t, TOK), :], q_rows, (((1,), (1,)), ((), ())),
                    preferred_element_type=jnp.float32,
                )
                score[j] = s
                part = fold(s, jnp.max)
                top = part if top is None else jnp.maximum(top, part)
            top = jnp.max(top, axis=0, keepdims=True)
            total = delta = None
            for j, t in enumerate(blocks):
                weight = jnp.exp2((score[j] - top) * exponent)
                score[j] = weight
                d = jnp.dot(v[aligned(t, TOK), :], g_cols, preferred_element_type=jnp.float32)
                prob_grad[j] = d
                one, two = fold(weight, jnp.sum), fold(weight * d, jnp.sum)
                total = one if total is None else total + one
                delta = two if delta is None else delta + two
            inverse = 1.0 / jnp.sum(total, axis=0, keepdims=True)
            delta = jnp.sum(delta, axis=0, keepdims=True) * inverse
            q_sum = None
            for j, t in enumerate(blocks):
                probs = score[j] * inverse
                probs_low = probs.astype(jnp.bfloat16)
                score_low = (probs * (prob_grad[j] - delta)).astype(jnp.bfloat16)
                at = aligned(t, TOK)
                dv_sum[at, :] += jnp.dot(probs_low, g_rows, preferred_element_type=jnp.float32)
                dk_sum[at, :] += jnp.dot(score_low, q_rows, preferred_element_type=jnp.float32)
                part = jnp.dot(k_turned[t], score_low, preferred_element_type=jnp.float32)
                q_sum = part if q_sum is None else q_sum + part
            dq[aligned(i, TOK), :] = (q_sum.T * scale).astype(jnp.bfloat16)

        for n in range(1, 9):
            pl.when(counts[0, i] == n)(functools.partial(run, n))
        return carry

    lax.fori_loop(0, NBLK, query_block, 0)
    dk[...] = (dk_sum[...] * scale).astype(jnp.bfloat16)
    dv[...] = dv_sum[...].astype(jnp.bfloat16)


def attention_grads(lists, counts, q, k, v, gt):
    heads = jax.ShapeDtypeStruct((NBLK * TOK, HD), jnp.bfloat16)
    scalars = pl.BlockSpec(memory_space=pltpu.SMEM)
    whole = pl.BlockSpec(memory_space=pltpu.VMEM)
    return pl.pallas_call(
        attention_kernel,
        name="attention_grads",
        out_shape=[heads] * 3,
        in_specs=[scalars] * 2 + [whole] * 4,
        out_specs=[whole] * 3,
        scratch_shapes=[
            pltpu.VMEM((NBLK, HD, TOK), jnp.bfloat16),
            pltpu.VMEM((8, TOK, TOK), jnp.float32),
            pltpu.VMEM((8, TOK, TOK), jnp.float32),
            pltpu.VMEM((NBLK * TOK, HD), jnp.float32),
            pltpu.VMEM((NBLK * TOK, HD), jnp.float32),
        ],
        compiler_params=pltpu.CompilerParams(vmem_limit_bytes=24 << 20),
    )(lists, counts, q, k, v, gt)


def scatter_kernel(*refs):
    ins, outs = refs[:3], refs[3:6]
    send_sem, recv_sem, local_sem = refs[6:]
    seq, dp = lax.axis_index("seq"), lax.axis_index("dp")
    peers = plane_peers(seq)
    enter([(p, dp) for p in peers])
    copies = []
    for n, (src, dst) in enumerate(zip(ins, outs)):
        for m, p in enumerate(peers):
            copies.append(remote(
                src.at[aligned(p, TOK), :], dst.at[:, aligned(seq, HD)],
                send_sem.at[n, m], recv_sem.at[n, m], (p, dp),
            ))
            copies[-1].start()
    for n, (src, dst) in enumerate(zip(ins, outs)):
        copies.append(pltpu.make_async_copy(
            src.at[aligned(seq, TOK), :], dst.at[:, aligned(seq, HD)], local_sem.at[n]
        ))
        copies[-1].start()
    for copy in copies:
        copy.wait()


def scatter_heads(dq, dk, dv):
    dma = pltpu.SemaphoreType.DMA
    anywhere = pl.BlockSpec(memory_space=pl.ANY)
    return pl.pallas_call(
        scatter_kernel,
        name="scatter_heads",
        out_shape=[jax.ShapeDtypeStruct((TOK, NS * HD), jnp.bfloat16)] * 3,
        in_specs=[anywhere] * 3,
        out_specs=[anywhere] * 3,
        scratch_shapes=[dma((3, len(OFFSETS))), dma((3, len(OFFSETS))), dma((3,))],
        compiler_params=pltpu.CompilerParams(
            collective_id=1, has_side_effects=True, vmem_limit_bytes=24 << 20
        ),
    )(dq, dk, dv)


def local(queries, key_states, value_states, grad_out, out_weight, block_lists, block_counts):
    flat = [a.reshape(a.shape[1:]) for a in (queries, key_states, value_states, grad_out)]
    q, k, v, gt = gather_heads(*flat, out_weight)
    grads = attention_grads(block_lists, block_counts, q, k, v, gt)
    return tuple(out[None] for out in scatter_heads(*grads))


def solution(mesh):
    tokens = P("dp", "seq", None)
    return jax.shard_map(
        local,
        mesh=mesh,
        in_specs=(tokens,) * 4 + (P("dp", None), P("seq", None, None), P("seq", None)),
        out_specs=(tokens,) * 3,
        check_vma=False,
    )
```

```python
import functools

import jax
import jax.numpy as jnp
from jax import lax
from jax.experimental import pallas as pl
from jax.experimental.pallas import tpu as pltpu
from jax.sharding import PartitionSpec as P

MESH = pl.DeviceIdType.MESH
HD = 128
NS = 16
NZ = 16
NBLK = 16
KMAX = 8
PAIRS = 64
UNROLL = 4
TOK = 128
HALF = HD // 2
PIECES = 2
PROWS = HALF // 2 // PIECES
FWD, BWD = 0, 1
PROJECTS = {4: (1,), 5: (2, 3), 6: (4, 5), 7: (6,), 8: (7,)}
GATHER_VMEM = 24 << 20
HOPS = (NZ // 2, NZ // 2 - 1)
OFFSETS = (
    (1, 0), (3, 0), (0, 1), (0, 3), (1, 1), (3, 3), (1, 3), (3, 1),
    (2, 0), (0, 2), (2, 1), (2, 3), (1, 2), (3, 2), (2, 2),
)


def aligned(index, size):
    return pl.ds(pl.multiple_of(index * size, size), size)


def plane_peers(seq):
    y, x = seq // 4, seq % 4
    return [((y + dy) % 4) * 4 + (x + dx) % 4 for dx, dy in OFFSETS]


def enter(devices):
    barrier = pltpu.get_barrier_semaphore()
    for device in devices:
        pl.semaphore_signal(barrier, inc=1, device_id=device, device_id_type=MESH)
    pl.semaphore_wait(barrier, len(devices))


def remote(src, dst, send_sem, recv_sem, device):
    return pltpu.make_async_remote_copy(
        src_ref=src, dst_ref=dst, send_sem=send_sem, recv_sem=recv_sem,
        device_id=device, device_id_type=MESH,
    )


def weight_rows(hop, way):
    if hop == 0:
        return 0, 0
    if hop == NZ // 2:
        return 0, HALF
    return hop, way * HALF


def gather_kernel(
    q_in, k_in, v_in, g_in, w_in, q_out, k_out, v_out, gt_out,
    rows, weights, product,
    head_send, head_recv, head_local, row_send, row_recv, row_local,
    w_local, w_send0, own_send, own_recv, w_send, w_recv, core_send, core_recv,
    g_send, g_recv, g_local,
):
    seq, dp = lax.axis_index("seq"), lax.axis_index("dp")
    z, core = dp // 2, dp % 2
    side = seq % 2
    pair = seq + 1 - 2 * side
    partner = (seq, z * 2 + 1 - core)
    peers = plane_peers(seq)

    def along(way, c):
        step = 1 if way == FWD else NZ - 1
        return (seq, ((z + step) % NZ) * 2 + c)

    enter(
        [(p, dp) for p in peers]
        + [partner]
        + [along(way, c) for way in (FWD, BWD) for c in (0, 1)]
    )

    def first_copies():
        copies = []
        for piece in range(PIECES):
            for way in (FWD, BWD):
                slot, base = weight_rows(1, way)
                for c in (0, 1):
                    at = c * (HALF // 2) + piece * PROWS
                    copies.append(remote(
                        w_in.at[pl.ds(at, PROWS), :],
                        weights.at[slot, pl.ds(base + at, PROWS), :],
                        w_send0.at[way, c, piece], w_recv.at[way, 1, piece],
                        along(way, c),
                    ))
        copies.append(remote(
            w_in, weights.at[0, pl.ds(0, HALF), :], own_send, own_recv, partner
        ))
        return copies

    own_copy = pltpu.make_async_copy(w_in, weights.at[0, pl.ds(0, HALF), :], w_local)

    @pl.when(core == side)
    def _():
        for copy in first_copies():
            copy.start()
        own_copy.start()

    row_copy = remote(
        g_in, rows.at[aligned(side, TOK), :], row_send, row_recv, (pair, dp)
    )
    row_copy.start()
    row_here = pltpu.make_async_copy(g_in, rows.at[aligned(side, TOK), :], row_local)
    row_here.start()

    head_copies, head_here = [], []
    for n, (src, dst) in enumerate(((q_in, q_out), (k_in, k_out), (v_in, v_out))):
        copy = pltpu.make_async_copy(
            src.at[:, aligned(seq, HD)], dst.at[aligned(seq, TOK), :], head_local.at[n]
        )
        copy.start()
        head_here.append(copy)
        for m, p in enumerate(peers):
            copy = remote(
                src.at[:, aligned(p, HD)], dst.at[aligned(seq, TOK), :],
                head_send.at[n, m], head_recv.at[n, m], (p, dp),
            )
            copy.start()
            head_copies.append(copy)

    def quarter(hop, way, c, piece):
        slot, base = weight_rows(hop, way)
        at = base + piece * PROWS + c * (HALF // 2)
        return weights.at[slot, pl.ds(pl.multiple_of(at, PROWS), PROWS), :]

    def onward(hop, way, piece):
        return remote(
            quarter(hop, way, core, piece), quarter(hop + 1, way, core, piece),
            w_send.at[way, hop, piece], w_recv.at[way, hop + 1, piece],
            along(way, core),
        )

    def arrival(hop, way, piece):
        here = quarter(hop, way, core, piece)
        return remote(
            here, here, w_send.at[way, hop, piece], w_recv.at[way, hop, piece],
            along(way, core),
        )

    def across(hop, way, piece):
        here = quarter(hop, way, core, piece)
        return remote(
            here, here, core_send.at[way, hop, piece], core_recv.at[way, hop, piece],
            partner,
        )

    def head_send_copy(slot, way, owner):
        return remote(
            product.at[slot, pl.ds(way * HALF, HALF), :],
            gt_out.at[aligned(side, HALF), aligned(seq // 2, 2 * TOK)],
            g_send.at[slot, way], g_recv.at[seq], (owner, dp),
        )

    def head_local_copy(slot, way):
        return pltpu.make_async_copy(
            product.at[slot, pl.ds(way * HALF, HALF), :],
            gt_out.at[aligned(side, HALF), aligned(seq // 2, 2 * TOK)],
            g_local,
        )

    def owners(slot):
        if slot == 0:
            return z, (z + NZ // 2) % NZ
        return (z + NZ - slot) % NZ, (z + slot) % NZ

    def project(slot, ways):
        span = pl.ds(ways[0] * HALF, len(ways) * HALF)
        product[slot, span, :] = lax.dot_general(
            weights[slot, span, :], rows[...], (((1,), (1,)), ((), ())),
            preferred_element_type=jnp.float32,
        ).astype(jnp.bfloat16)
        for way in ways:
            owner = owners(slot)[way]

            @pl.when(owner != seq)
            def _(way=way, owner=owner):
                head_send_copy(slot, way, owner).start()

            @pl.when(owner == seq)
            def _(way=way):
                head_local_copy(slot, way).start()

    for hop in range(1, NZ // 2 + 1):
        ways = [way for way in (FWD, BWD) if hop <= HOPS[way]]
        for piece in range(PIECES):
            for way in ways:
                arrival(hop, way, piece).wait_recv()
                if hop < HOPS[way]:
                    onward(hop, way, piece).start()
                across(hop, way, piece).start()
        if hop == min(PROJECTS):
            row_here.wait()
            row_copy.wait_recv()

            @pl.when(core == side)
            def _():
                own_copy.wait()

            @pl.when(core != side)
            def _():
                remote(
                    w_in, weights.at[0, pl.ds(0, HALF), :], own_send, own_recv, partner
                ).wait_recv()

            project(0, (FWD,))
        for slot in PROJECTS.get(hop, ()):
            for piece in range(PIECES):
                for way in (FWD, BWD):
                    across(slot, way, piece).wait_recv()
            project(slot, (FWD, BWD))
    for piece in range(PIECES):
        across(NZ // 2, FWD, piece).wait_recv()
    project(0, (BWD,))

    @pl.when(core == side)
    def _():
        for copy in first_copies():
            copy.wait_send()

    for hop in range(1, NZ // 2 + 1):
        for piece in range(PIECES):
            for way in (FWD, BWD):
                if hop < HOPS[way]:
                    onward(hop, way, piece).wait_send()
                if hop <= HOPS[way]:
                    across(hop, way, piece).wait_send()
    row_copy.wait_send()
    for copy in head_here:
        copy.wait()
    for copy in head_copies:
        copy.wait()
    for slot in range(NZ // 2):
        for way, owner in enumerate(owners(slot)):
            @pl.when(owner != seq)
            def _(slot=slot, way=way, owner=owner):
                head_send_copy(slot, way, owner).wait_send()

            @pl.when(owner == seq)
            def _(slot=slot, way=way):
                head_local_copy(slot, way).wait()
    for other in range(NS):
        @pl.when(other != seq)
        def _(other=other):
            block = gt_out.at[pl.ds(0, HALF), pl.ds(0, 2 * TOK)]
            remote(
                block, block, g_send.at[0, 0], g_recv.at[other], (other, dp)
            ).wait_recv()


def gather_heads(q, k, v, g, w):
    dma = pltpu.SemaphoreType.DMA
    heads = jax.ShapeDtypeStruct((NS * TOK, HD), jnp.bfloat16)
    turned = jax.ShapeDtypeStruct((HD, NS * TOK), jnp.bfloat16)
    width = g.shape[1]
    anywhere = pl.BlockSpec(memory_space=pl.ANY)
    hops = NZ // 2 + 1
    return pl.pallas_call(
        gather_kernel,
        name="gather_heads",
        out_shape=[heads, heads, heads, turned],
        in_specs=[anywhere] * 5,
        out_specs=[anywhere] * 4,
        scratch_shapes=[
            pltpu.VMEM((2 * TOK, width), jnp.bfloat16),
            pltpu.VMEM((NZ // 2, HD, width), jnp.bfloat16),
            pltpu.VMEM((NZ // 2, HD, 2 * TOK), jnp.bfloat16),
            dma((3, len(OFFSETS))), dma((3, len(OFFSETS))), dma((3,)),
            dma, dma, dma,
            dma, dma((2, 2, PIECES)), dma, dma,
            dma((2, hops, PIECES)), dma((2, hops, PIECES)),
            dma((2, hops, PIECES)), dma((2, hops, PIECES)),
            dma((NZ // 2, 2)), dma((NS,)), dma,
        ],
        compiler_params=pltpu.CompilerParams(
            collective_id=0, has_side_effects=True, vmem_limit_bytes=GATHER_VMEM
        ),
    )(q, k, v, g, w)


def attention_kernel(
    lists, counts, q, k, v, gt, dq, dk, dv,
    pair_q, pair_k, k_turned, g_rows, score, prob_grad, top, total, delta,
    dq_sum, dk_sum, dv_sum,
):
    scale = HD ** -0.5
    exponent = scale * 1.4426950408889634

    used = jnp.int32(0)
    for i in range(NBLK):
        for j in range(KMAX):
            pair_q[used + j] = jnp.int32(i)
            pair_k[used + j] = lists[0, j, i]
        used = used + counts[0, i]
    steps = (used + UNROLL - 1) // UNROLL

    dk_sum[...] = jnp.zeros_like(dk_sum)
    dv_sum[...] = jnp.zeros_like(dv_sum)
    dq_sum[...] = jnp.zeros_like(dq_sum)
    top[...] = jnp.full_like(top, -1e30)
    total[...] = jnp.zeros_like(total)
    delta[...] = jnp.zeros_like(delta)
    for t in range(NBLK):
        k_turned[t] = k[pl.ds(t * TOK, TOK), :].T
        g_rows[t] = gt[:, pl.ds(t * TOK, TOK)].T

    def tiles(x):
        return x.reshape(TOK // 8, 8, TOK)

    def each_pair(body):
        def step(n, carry):
            for m in range(UNROLL):
                t = n * UNROLL + m
                body(t, pair_q[t], pair_k[t])
            return carry

        lax.fori_loop(0, steps, step, 0)

    def scores(t, i, b):
        s = lax.dot_general(
            k[aligned(b, TOK), :], q[aligned(i, TOK), :], (((1,), (1,)), ((), ())),
            preferred_element_type=jnp.float32,
        )
        s = tiles(s) + jnp.where(t < used, 0.0, -1e30)
        score[t] = s
        top[i] = jnp.maximum(top[i], jnp.max(s, axis=0))
        prob_grad[t] = tiles(jnp.dot(
            v[aligned(b, TOK), :], gt[:, aligned(i, TOK)], preferred_element_type=jnp.float32
        ))

    each_pair(scores)
    top[...] = jnp.broadcast_to(
        jnp.max(top[...], axis=1, keepdims=True) * exponent, top.shape
    )

    def weigh(t, i, b):
        weight = jnp.exp2(score[t] * exponent - top[i])
        score[t] = weight
        total[i] += jnp.sum(weight, axis=0)
        delta[i] += jnp.sum(weight * prob_grad[t], axis=0)

    each_pair(weigh)
    inverse = 1.0 / jnp.sum(total[...], axis=1, keepdims=True)
    delta[...] = jnp.broadcast_to(
        jnp.sum(delta[...], axis=1, keepdims=True) * inverse, delta.shape
    )
    total[...] = jnp.broadcast_to(inverse, total.shape)

    def gradients(t, i, b):
        probs = score[t] * total[i]
        probs_low = probs.reshape(TOK, TOK).astype(jnp.bfloat16)
        score_low = (probs * (prob_grad[t] - delta[i])).reshape(TOK, TOK).astype(jnp.bfloat16)
        dv_sum[b] += jnp.dot(probs_low, g_rows[i], preferred_element_type=jnp.float32)
        dk_sum[b] += jnp.dot(
            score_low, q[aligned(i, TOK), :], preferred_element_type=jnp.float32
        )
        dq_sum[i] += jnp.dot(k_turned[b], score_low, preferred_element_type=jnp.float32)

    each_pair(gradients)
    for t in range(NBLK):
        rows = pl.ds(t * TOK, TOK)
        dq[rows, :] = (dq_sum[t].T * scale).astype(jnp.bfloat16)
        dk[rows, :] = (dk_sum[t] * scale).astype(jnp.bfloat16)
        dv[rows, :] = dv_sum[t].astype(jnp.bfloat16)


def attention_grads(lists, counts, q, k, v, gt):
    heads = jax.ShapeDtypeStruct((NBLK * TOK, HD), jnp.bfloat16)
    scalars = pl.BlockSpec(memory_space=pltpu.SMEM)
    whole = pl.BlockSpec(memory_space=pltpu.VMEM)
    blocks = (NBLK, TOK, HD)
    return pl.pallas_call(
        attention_kernel,
        name="attention_grads",
        out_shape=[heads] * 3,
        in_specs=[scalars] * 2 + [whole] * 4,
        out_specs=[whole] * 3,
        scratch_shapes=[
            pltpu.SMEM((PAIRS + KMAX,), jnp.int32),
            pltpu.SMEM((PAIRS + KMAX,), jnp.int32),
            pltpu.VMEM(blocks, jnp.bfloat16),
            pltpu.VMEM(blocks, jnp.bfloat16),
            pltpu.VMEM((PAIRS, TOK // 8, 8, TOK), jnp.float32),
            pltpu.VMEM((PAIRS, TOK // 8, 8, TOK), jnp.float32),
            pltpu.VMEM((NBLK, 8, TOK), jnp.float32),
            pltpu.VMEM((NBLK, 8, TOK), jnp.float32),
            pltpu.VMEM((NBLK, 8, TOK), jnp.float32),
            pltpu.VMEM(blocks, jnp.float32),
            pltpu.VMEM(blocks, jnp.float32),
            pltpu.VMEM(blocks, jnp.float32),
        ],
        compiler_params=pltpu.CompilerParams(vmem_limit_bytes=32 << 20),
    )(lists, counts, q, k, v, gt)


def scatter_kernel(*refs):
    ins, outs = refs[:3], refs[3:6]
    send_sem, recv_sem, local_sem = refs[6:]
    seq, dp = lax.axis_index("seq"), lax.axis_index("dp")
    peers = plane_peers(seq)
    enter([(p, dp) for p in peers])
    copies = []
    for n, (src, dst) in enumerate(zip(ins, outs)):
        for m, p in enumerate(peers):
            copies.append(remote(
                src.at[aligned(p, TOK), :], dst.at[:, aligned(seq, HD)],
                send_sem.at[n, m], recv_sem.at[n, m], (p, dp),
            ))
            copies[-1].start()
    for n, (src, dst) in enumerate(zip(ins, outs)):
        copies.append(pltpu.make_async_copy(
            src.at[aligned(seq, TOK), :], dst.at[:, aligned(seq, HD)], local_sem.at[n]
        ))
        copies[-1].start()
    for copy in copies:
        copy.wait()


def scatter_heads(dq, dk, dv):
    dma = pltpu.SemaphoreType.DMA
    anywhere = pl.BlockSpec(memory_space=pl.ANY)
    return pl.pallas_call(
        scatter_kernel,
        name="scatter_heads",
        out_shape=[jax.ShapeDtypeStruct((TOK, NS * HD), jnp.bfloat16)] * 3,
        in_specs=[anywhere] * 3,
        out_specs=[anywhere] * 3,
        scratch_shapes=[dma((3, len(OFFSETS))), dma((3, len(OFFSETS))), dma((3,))],
        compiler_params=pltpu.CompilerParams(
            collective_id=1, has_side_effects=True, vmem_limit_bytes=24 << 20
        ),
    )(dq, dk, dv)


def store_kernel(*refs):
    copies = [
        pltpu.make_async_copy(src, dst, refs[6].at[n])
        for n, (src, dst) in enumerate(zip(refs[:3], refs[3:6]))
    ]
    for copy in copies:
        copy.start()
    for copy in copies:
        copy.wait()


def store_results(*arrays):
    anywhere = pl.BlockSpec(memory_space=pl.ANY)
    return pl.pallas_call(
        store_kernel,
        name="store_results",
        out_shape=[jax.ShapeDtypeStruct(a.shape, a.dtype) for a in arrays],
        in_specs=[anywhere] * 3,
        out_specs=[anywhere] * 3,
        scratch_shapes=[pltpu.SemaphoreType.DMA((3,))],
        compiler_params=pltpu.CompilerParams(vmem_limit_bytes=24 << 20),
    )(*arrays)


def local(queries, key_states, value_states, grad_out, out_weight, block_lists, block_counts):
    flat = [a.reshape(a.shape[1:]) for a in (queries, key_states, value_states, grad_out)]
    held = [pltpu.with_memory_space_constraint(a, pltpu.HBM) for a in (*flat, out_weight)]
    q, k, v, gt = gather_heads(*held)
    grads = attention_grads(jnp.swapaxes(block_lists, 1, 2), block_counts, q, k, v, gt)
    return tuple(out[None] for out in store_results(*scatter_heads(*grads)))


def solution(mesh):
    tokens = P("dp", "seq", None)
    return jax.shard_map(
        local,
        mesh=mesh,
        in_specs=(tokens,) * 4 + (P("dp", None), P("seq", None, None), P("seq", None)),
        out_specs=(tokens,) * 3,
        check_vma=False,
    )
```

```python
import functools

import jax
import jax.numpy as jnp
from jax import lax
from jax.experimental import pallas as pl
from jax.experimental.pallas import tpu as pltpu
from jax.sharding import PartitionSpec as P

MESH = pl.DeviceIdType.MESH
HD = 128
NS = 16
NZ = 16
NBLK = 16
KMAX = 8
PAIRS = 64
UNROLL = 32
TOK = 128
HALF = HD // 2
PIECES = 2
PROWS = HALF // 2 // PIECES
FWD, BWD = 0, 1
PROJECTS = {4: (1,), 5: (2, 3), 6: (4, 5), 7: (6,), 8: (7,)}
GATHER_VMEM = 24 << 20
HOPS = (NZ // 2, NZ // 2 - 1)
OFFSETS = (
    (1, 0), (3, 0), (0, 1), (0, 3), (1, 1), (3, 3), (1, 3), (3, 1),
    (2, 0), (0, 2), (2, 1), (2, 3), (1, 2), (3, 2), (2, 2),
)


def aligned(index, size):
    return pl.ds(pl.multiple_of(index * size, size), size)


def plane_peers(seq):
    y, x = seq // 4, seq % 4
    return [((y + dy) % 4) * 4 + (x + dx) % 4 for dx, dy in OFFSETS]


def enter(devices):
    barrier = pltpu.get_barrier_semaphore()
    for device in devices:
        pl.semaphore_signal(barrier, inc=1, device_id=device, device_id_type=MESH)
    pl.semaphore_wait(barrier, len(devices))


def remote(src, dst, send_sem, recv_sem, device):
    return pltpu.make_async_remote_copy(
        src_ref=src, dst_ref=dst, send_sem=send_sem, recv_sem=recv_sem,
        device_id=device, device_id_type=MESH,
    )


def weight_rows(hop, way):
    if hop == 0:
        return 0, 0
    if hop == NZ // 2:
        return 0, HALF
    return hop, way * HALF


def gather_kernel(
    q_in, k_in, v_in, g_in, w_in, q_out, k_out, v_out, gt_out,
    rows, weights, product,
    head_send, head_recv, head_local, row_send, row_recv, row_local,
    w_local, w_send0, own_send, own_recv, w_send, w_recv, core_send, core_recv,
    g_send, g_recv, g_local,
):
    seq, dp = lax.axis_index("seq"), lax.axis_index("dp")
    z, core = dp // 2, dp % 2
    side = seq % 2
    pair = seq + 1 - 2 * side
    partner = (seq, z * 2 + 1 - core)
    peers = plane_peers(seq)

    def along(way, c):
        step = 1 if way == FWD else NZ - 1
        return (seq, ((z + step) % NZ) * 2 + c)

    enter(
        [(p, dp) for p in peers]
        + [partner]
        + [along(way, c) for way in (FWD, BWD) for c in (0, 1)]
    )

    def first_copies():
        copies = []
        for piece in range(PIECES):
            for way in (FWD, BWD):
                slot, base = weight_rows(1, way)
                for c in (0, 1):
                    at = c * (HALF // 2) + piece * PROWS
                    copies.append(remote(
                        w_in.at[pl.ds(at, PROWS), :],
                        weights.at[slot, pl.ds(base + at, PROWS), :],
                        w_send0.at[way, c, piece], w_recv.at[way, 1, piece],
                        along(way, c),
                    ))
        copies.append(remote(
            w_in, weights.at[0, pl.ds(0, HALF), :], own_send, own_recv, partner
        ))
        return copies

    own_copy = pltpu.make_async_copy(w_in, weights.at[0, pl.ds(0, HALF), :], w_local)

    @pl.when(core == side)
    def _():
        for copy in first_copies():
            copy.start()
        own_copy.start()

    row_copy = remote(
        g_in, rows.at[aligned(side, TOK), :], row_send, row_recv, (pair, dp)
    )
    row_copy.start()
    row_here = pltpu.make_async_copy(g_in, rows.at[aligned(side, TOK), :], row_local)
    row_here.start()

    head_copies, head_here = [], []
    for n, (src, dst) in enumerate(((q_in, q_out), (k_in, k_out), (v_in, v_out))):
        copy = pltpu.make_async_copy(
            src.at[:, aligned(seq, HD)], dst.at[aligned(seq, TOK), :], head_local.at[n]
        )
        copy.start()
        head_here.append(copy)
        for m, p in enumerate(peers):
            copy = remote(
                src.at[:, aligned(p, HD)], dst.at[aligned(seq, TOK), :],
                head_send.at[n, m], head_recv.at[n, m], (p, dp),
            )
            copy.start()
            head_copies.append(copy)

    def quarter(hop, way, c, piece):
        slot, base = weight_rows(hop, way)
        at = base + piece * PROWS + c * (HALF // 2)
        return weights.at[slot, pl.ds(pl.multiple_of(at, PROWS), PROWS), :]

    def onward(hop, way, piece):
        return remote(
            quarter(hop, way, core, piece), quarter(hop + 1, way, core, piece),
            w_send.at[way, hop, piece], w_recv.at[way, hop + 1, piece],
            along(way, core),
        )

    def arrival(hop, way, piece):
        here = quarter(hop, way, core, piece)
        return remote(
            here, here, w_send.at[way, hop, piece], w_recv.at[way, hop, piece],
            along(way, core),
        )

    def across(hop, way, piece):
        here = quarter(hop, way, core, piece)
        return remote(
            here, here, core_send.at[way, hop, piece], core_recv.at[way, hop, piece],
            partner,
        )

    def head_send_copy(slot, way, owner):
        return remote(
            product.at[slot, pl.ds(way * HALF, HALF), :],
            gt_out.at[aligned(side, HALF), aligned(seq // 2, 2 * TOK)],
            g_send.at[slot, way], g_recv.at[seq], (owner, dp),
        )

    def head_local_copy(slot, way):
        return pltpu.make_async_copy(
            product.at[slot, pl.ds(way * HALF, HALF), :],
            gt_out.at[aligned(side, HALF), aligned(seq // 2, 2 * TOK)],
            g_local,
        )

    def owners(slot):
        if slot == 0:
            return z, (z + NZ // 2) % NZ
        return (z + NZ - slot) % NZ, (z + slot) % NZ

    def project(slot, ways):
        span = pl.ds(ways[0] * HALF, len(ways) * HALF)
        product[slot, span, :] = lax.dot_general(
            weights[slot, span, :], rows[...], (((1,), (1,)), ((), ())),
            preferred_element_type=jnp.float32,
        ).astype(jnp.bfloat16)
        for way in ways:
            owner = owners(slot)[way]

            @pl.when(owner != seq)
            def _(way=way, owner=owner):
                head_send_copy(slot, way, owner).start()

            @pl.when(owner == seq)
            def _(way=way):
                head_local_copy(slot, way).start()

    for hop in range(1, NZ // 2 + 1):
        ways = [way for way in (FWD, BWD) if hop <= HOPS[way]]
        for piece in range(PIECES):
            for way in ways:
                arrival(hop, way, piece).wait_recv()
                if hop < HOPS[way]:
                    onward(hop, way, piece).start()
                across(hop, way, piece).start()
        if hop == min(PROJECTS):
            row_here.wait()
            row_copy.wait_recv()

            @pl.when(core == side)
            def _():
                own_copy.wait()

            @pl.when(core != side)
            def _():
                remote(
                    w_in, weights.at[0, pl.ds(0, HALF), :], own_send, own_recv, partner
                ).wait_recv()

            project(0, (FWD,))
        for slot in PROJECTS.get(hop, ()):
            for piece in range(PIECES):
                for way in (FWD, BWD):
                    across(slot, way, piece).wait_recv()
            project(slot, (FWD, BWD))
    for piece in range(PIECES):
        across(NZ // 2, FWD, piece).wait_recv()
    project(0, (BWD,))

    @pl.when(core == side)
    def _():
        for copy in first_copies():
            copy.wait_send()

    for hop in range(1, NZ // 2 + 1):
        for piece in range(PIECES):
            for way in (FWD, BWD):
                if hop < HOPS[way]:
                    onward(hop, way, piece).wait_send()
                if hop <= HOPS[way]:
                    across(hop, way, piece).wait_send()
    row_copy.wait_send()
    for copy in head_here:
        copy.wait()
    for copy in head_copies:
        copy.wait()
    for slot in range(NZ // 2):
        for way, owner in enumerate(owners(slot)):
            @pl.when(owner != seq)
            def _(slot=slot, way=way, owner=owner):
                head_send_copy(slot, way, owner).wait_send()

            @pl.when(owner == seq)
            def _(slot=slot, way=way):
                head_local_copy(slot, way).wait()
    for other in range(NS):
        @pl.when(other != seq)
        def _(other=other):
            block = gt_out.at[pl.ds(0, HALF), pl.ds(0, 2 * TOK)]
            remote(
                block, block, g_send.at[0, 0], g_recv.at[other], (other, dp)
            ).wait_recv()


def gather_heads(q, k, v, g, w):
    dma = pltpu.SemaphoreType.DMA
    heads = jax.ShapeDtypeStruct((NS * TOK, HD), jnp.bfloat16)
    turned = jax.ShapeDtypeStruct((HD, NS * TOK), jnp.bfloat16)
    width = g.shape[1]
    anywhere = pl.BlockSpec(memory_space=pl.ANY)
    hops = NZ // 2 + 1
    return pl.pallas_call(
        gather_kernel,
        name="gather_heads",
        out_shape=[heads, heads, heads, turned],
        in_specs=[anywhere] * 5,
        out_specs=[anywhere] * 4,
        scratch_shapes=[
            pltpu.VMEM((2 * TOK, width), jnp.bfloat16),
            pltpu.VMEM((NZ // 2, HD, width), jnp.bfloat16),
            pltpu.VMEM((NZ // 2, HD, 2 * TOK), jnp.bfloat16),
            dma((3, len(OFFSETS))), dma((3, len(OFFSETS))), dma((3,)),
            dma, dma, dma,
            dma, dma((2, 2, PIECES)), dma, dma,
            dma((2, hops, PIECES)), dma((2, hops, PIECES)),
            dma((2, hops, PIECES)), dma((2, hops, PIECES)),
            dma((NZ // 2, 2)), dma((NS,)), dma,
        ],
        compiler_params=pltpu.CompilerParams(
            collective_id=0, has_side_effects=True, vmem_limit_bytes=GATHER_VMEM
        ),
    )(q, k, v, g, w)


def attention_kernel(
    lists, counts, q, k, v, gt, dq, dk, dv,
    pair_q, pair_k, k_turned, g_rows, score, prob_grad, top, total, delta,
    dq_sum, dk_sum, dv_sum,
):
    scale = HD ** -0.5
    exponent = scale * 1.4426950408889634

    used = jnp.int32(0)
    for i in range(NBLK):
        for j in range(KMAX):
            pair_q[used + j] = jnp.int32(i)
            pair_k[used + j] = lists[0, j, i]
        used = used + counts[0, i]
    for m in range(UNROLL):
        pair_q[used + m] = jnp.int32(0)
        pair_k[used + m] = jnp.int32(0)
    steps = (used + UNROLL - 1) // UNROLL

    dk_sum[...] = jnp.zeros_like(dk_sum)
    dv_sum[...] = jnp.zeros_like(dv_sum)
    dq_sum[...] = jnp.zeros_like(dq_sum)
    top[...] = jnp.full_like(top, -1e30)
    total[...] = jnp.zeros_like(total)
    delta[...] = jnp.zeros_like(delta)
    for t in range(NBLK):
        k_turned[t] = k[pl.ds(t * TOK, TOK), :].T
        g_rows[t] = gt[:, pl.ds(t * TOK, TOK)].T

    def tiles(x):
        return x.reshape(TOK // 8, 8, TOK)

    def each_pair(body):
        def step(n, carry):
            for m in range(UNROLL):
                t = n * UNROLL + m
                body(t, pair_q[t], pair_k[t])
            return carry

        lax.fori_loop(0, steps, step, 0)

    def scores(t, i, b):
        s = lax.dot_general(
            k[aligned(b, TOK), :], q[aligned(i, TOK), :], (((1,), (1,)), ((), ())),
            preferred_element_type=jnp.float32,
        )
        s = tiles(s) + jnp.where(t < used, 0.0, -1e30)
        score[t] = s
        top[i] = jnp.maximum(top[i], jnp.max(s, axis=0))
        prob_grad[t] = tiles(jnp.dot(
            v[aligned(b, TOK), :], gt[:, aligned(i, TOK)], preferred_element_type=jnp.float32
        ))

    each_pair(scores)
    top[...] = jnp.broadcast_to(
        jnp.max(top[...], axis=1, keepdims=True) * exponent, top.shape
    )

    def weigh(t, i, b):
        weight = jnp.exp2(score[t] * exponent - top[i])
        score[t] = weight
        total[i] += jnp.sum(weight, axis=0)
        delta[i] += jnp.sum(weight * prob_grad[t], axis=0)

    each_pair(weigh)
    inverse = 1.0 / jnp.sum(total[...], axis=1, keepdims=True)
    delta[...] = jnp.broadcast_to(
        jnp.sum(delta[...], axis=1, keepdims=True) * inverse, delta.shape
    )
    total[...] = jnp.broadcast_to(inverse, total.shape)

    def gradients(t, i, b):
        probs = score[t] * total[i]
        probs_low = probs.reshape(TOK, TOK).astype(jnp.bfloat16)
        score_low = (probs * (prob_grad[t] - delta[i])).reshape(TOK, TOK).astype(jnp.bfloat16)
        dv_sum[b] += jnp.dot(probs_low, g_rows[i], preferred_element_type=jnp.float32)
        dk_sum[b] += jnp.dot(
            score_low, q[aligned(i, TOK), :], preferred_element_type=jnp.float32
        )
        dq_sum[i] += jnp.dot(k_turned[b], score_low, preferred_element_type=jnp.float32)

    each_pair(gradients)
    for t in range(NBLK):
        rows = pl.ds(t * TOK, TOK)
        dq[rows, :] = (dq_sum[t].T * scale).astype(jnp.bfloat16)
        dk[rows, :] = (dk_sum[t] * scale).astype(jnp.bfloat16)
        dv[rows, :] = dv_sum[t].astype(jnp.bfloat16)


def attention_grads(lists, counts, q, k, v, gt):
    heads = jax.ShapeDtypeStruct((NBLK * TOK, HD), jnp.bfloat16)
    scalars = pl.BlockSpec(memory_space=pltpu.SMEM)
    whole = pl.BlockSpec(memory_space=pltpu.VMEM)
    blocks = (NBLK, TOK, HD)
    return pl.pallas_call(
        attention_kernel,
        name="attention_grads",
        out_shape=[heads] * 3,
        in_specs=[scalars] * 2 + [whole] * 4,
        out_specs=[whole] * 3,
        scratch_shapes=[
            pltpu.SMEM((PAIRS + KMAX + UNROLL,), jnp.int32),
            pltpu.SMEM((PAIRS + KMAX + UNROLL,), jnp.int32),
            pltpu.VMEM(blocks, jnp.bfloat16),
            pltpu.VMEM(blocks, jnp.bfloat16),
            pltpu.VMEM((PAIRS, TOK // 8, 8, TOK), jnp.float32),
            pltpu.VMEM((PAIRS, TOK // 8, 8, TOK), jnp.float32),
            pltpu.VMEM((NBLK, 8, TOK), jnp.float32),
            pltpu.VMEM((NBLK, 8, TOK), jnp.float32),
            pltpu.VMEM((NBLK, 8, TOK), jnp.float32),
            pltpu.VMEM(blocks, jnp.float32),
            pltpu.VMEM(blocks, jnp.float32),
            pltpu.VMEM(blocks, jnp.float32),
        ],
        compiler_params=pltpu.CompilerParams(vmem_limit_bytes=32 << 20),
    )(lists, counts, q, k, v, gt)


def scatter_kernel(*refs):
    ins, outs = refs[:3], refs[3:6]
    send_sem, recv_sem, local_sem = refs[6:]
    seq, dp = lax.axis_index("seq"), lax.axis_index("dp")
    peers = plane_peers(seq)
    enter([(p, dp) for p in peers])
    copies = []
    for n, (src, dst) in enumerate(zip(ins, outs)):
        for m, p in enumerate(peers):
            copies.append(remote(
                src.at[aligned(p, TOK), :], dst.at[:, aligned(seq, HD)],
                send_sem.at[n, m], recv_sem.at[n, m], (p, dp),
            ))
            copies[-1].start()
    for n, (src, dst) in enumerate(zip(ins, outs)):
        copies.append(pltpu.make_async_copy(
            src.at[aligned(seq, TOK), :], dst.at[:, aligned(seq, HD)], local_sem.at[n]
        ))
        copies[-1].start()
    for copy in copies:
        copy.wait()


def scatter_heads(dq, dk, dv):
    dma = pltpu.SemaphoreType.DMA
    anywhere = pl.BlockSpec(memory_space=pl.ANY)
    return pl.pallas_call(
        scatter_kernel,
        name="scatter_heads",
        out_shape=[jax.ShapeDtypeStruct((TOK, NS * HD), jnp.bfloat16)] * 3,
        in_specs=[anywhere] * 3,
        out_specs=[anywhere] * 3,
        scratch_shapes=[dma((3, len(OFFSETS))), dma((3, len(OFFSETS))), dma((3,))],
        compiler_params=pltpu.CompilerParams(
            collective_id=1, has_side_effects=True, vmem_limit_bytes=24 << 20
        ),
    )(dq, dk, dv)


def store_kernel(*refs):
    copies = [
        pltpu.make_async_copy(src, dst, refs[6].at[n])
        for n, (src, dst) in enumerate(zip(refs[:3], refs[3:6]))
    ]
    for copy in copies:
        copy.start()
    for copy in copies:
        copy.wait()


def store_results(*arrays):
    anywhere = pl.BlockSpec(memory_space=pl.ANY)
    return pl.pallas_call(
        store_kernel,
        name="store_results",
        out_shape=[jax.ShapeDtypeStruct(a.shape, a.dtype) for a in arrays],
        in_specs=[anywhere] * 3,
        out_specs=[anywhere] * 3,
        scratch_shapes=[pltpu.SemaphoreType.DMA((3,))],
        compiler_params=pltpu.CompilerParams(vmem_limit_bytes=24 << 20),
    )(*arrays)


def local(queries, key_states, value_states, grad_out, out_weight, block_lists, block_counts):
    flat = [a.reshape(a.shape[1:]) for a in (queries, key_states, value_states, grad_out)]
    held = [pltpu.with_memory_space_constraint(a, pltpu.HBM) for a in (*flat, out_weight)]
    q, k, v, gt = gather_heads(*held)
    block_lists = pltpu.with_memory_space_constraint(jnp.swapaxes(block_lists, 1, 2), pltpu.HBM)
    block_counts = pltpu.with_memory_space_constraint(block_counts, pltpu.HBM)
    grads = attention_grads(block_lists, block_counts, q, k, v, gt)
    return tuple(out[None] for out in store_results(*scatter_heads(*grads)))


def solution(mesh):
    tokens = P("dp", "seq", None)
    return jax.shard_map(
        local,
        mesh=mesh,
        in_specs=(tokens,) * 4 + (P("dp", None), P("seq", None, None), P("seq", None)),
        out_specs=(tokens,) * 3,
        check_vma=False,
    )
```

```python
import functools

import jax
import jax.numpy as jnp
from jax import lax
from jax.experimental import pallas as pl
from jax.experimental.pallas import tpu as pltpu
from jax.sharding import PartitionSpec as P

MESH = pl.DeviceIdType.MESH
HD = 128
NS = 16
NZ = 16
NBLK = 16
KMAX = 8
PAIRS = 64
UNROLL = 32
TOK = 128
HALF = HD // 2
PIECES = 2
PROWS = HALF // 2 // PIECES
FWD, BWD = 0, 1
PROJECTS = {4: (1,), 5: (2, 3), 6: (4, 5), 7: (6,), 8: (7,)}
GATHER_VMEM = 24 << 20
HOPS = (NZ // 2, NZ // 2 - 1)
OFFSETS = (
    (1, 0), (3, 0), (0, 1), (0, 3), (1, 1), (3, 3), (1, 3), (3, 1),
    (2, 0), (0, 2), (2, 1), (2, 3), (1, 2), (3, 2), (2, 2),
)


def aligned(index, size):
    return pl.ds(pl.multiple_of(index * size, size), size)


def plane_peers(seq):
    y, x = seq // 4, seq % 4
    return [((y + dy) % 4) * 4 + (x + dx) % 4 for dx, dy in OFFSETS]


def enter(devices):
    barrier = pltpu.get_barrier_semaphore()
    for device in devices:
        pl.semaphore_signal(barrier, inc=1, device_id=device, device_id_type=MESH)
    pl.semaphore_wait(barrier, len(devices))


def remote(src, dst, send_sem, recv_sem, device):
    return pltpu.make_async_remote_copy(
        src_ref=src, dst_ref=dst, send_sem=send_sem, recv_sem=recv_sem,
        device_id=device, device_id_type=MESH,
    )


def weight_rows(hop, way):
    if hop == 0:
        return 0, 0
    if hop == NZ // 2:
        return 0, HALF
    return hop, way * HALF


def gather_kernel(
    q_in, k_in, v_in, g_in, w_in, q_out, k_out, v_out, gt_out,
    rows, weights, product,
    head_send, head_recv, head_local, row_send, row_recv, row_local,
    w_local, w_send0, own_send, own_recv, w_send, w_recv, core_send, core_recv,
    g_send, g_recv, g_local,
):
    seq, dp = lax.axis_index("seq"), lax.axis_index("dp")
    z, core = dp // 2, dp % 2
    side = seq % 2
    pair = seq + 1 - 2 * side
    partner = (seq, z * 2 + 1 - core)
    peers = plane_peers(seq)

    def along(way, c):
        step = 1 if way == FWD else NZ - 1
        return (seq, ((z + step) % NZ) * 2 + c)

    enter(
        [(p, dp) for p in peers]
        + [partner]
        + [along(way, c) for way in (FWD, BWD) for c in (0, 1)]
    )

    def first_copies():
        copies = []
        for piece in range(PIECES):
            for way in (FWD, BWD):
                slot, base = weight_rows(1, way)
                for c in (0, 1):
                    at = c * (HALF // 2) + piece * PROWS
                    copies.append(remote(
                        w_in.at[pl.ds(at, PROWS), :],
                        weights.at[slot, pl.ds(base + at, PROWS), :],
                        w_send0.at[way, c, piece], w_recv.at[way, 1, piece],
                        along(way, c),
                    ))
        copies.append(remote(
            w_in, weights.at[0, pl.ds(0, HALF), :], own_send, own_recv, partner
        ))
        return copies

    own_copy = pltpu.make_async_copy(w_in, weights.at[0, pl.ds(0, HALF), :], w_local)

    @pl.when(core == side)
    def _():
        for copy in first_copies():
            copy.start()
        own_copy.start()

    row_copy = remote(
        g_in, rows.at[aligned(side, TOK), :], row_send, row_recv, (pair, dp)
    )
    row_copy.start()
    row_here = pltpu.make_async_copy(g_in, rows.at[aligned(side, TOK), :], row_local)
    row_here.start()

    head_copies, head_here = [], []
    for n, (src, dst) in enumerate(((q_in, q_out), (k_in, k_out), (v_in, v_out))):
        copy = pltpu.make_async_copy(
            src.at[:, aligned(seq, HD)], dst.at[aligned(seq, TOK), :], head_local.at[n]
        )
        copy.start()
        head_here.append(copy)
        for m, p in enumerate(peers):
            copy = remote(
                src.at[:, aligned(p, HD)], dst.at[aligned(seq, TOK), :],
                head_send.at[n, m], head_recv.at[n, m], (p, dp),
            )
            copy.start()
            head_copies.append(copy)

    def quarter(hop, way, c, piece):
        slot, base = weight_rows(hop, way)
        at = base + piece * PROWS + c * (HALF // 2)
        return weights.at[slot, pl.ds(pl.multiple_of(at, PROWS), PROWS), :]

    def onward(hop, way, piece):
        return remote(
            quarter(hop, way, core, piece), quarter(hop + 1, way, core, piece),
            w_send.at[way, hop, piece], w_recv.at[way, hop + 1, piece],
            along(way, core),
        )

    def arrival(hop, way, piece):
        here = quarter(hop, way, core, piece)
        return remote(
            here, here, w_send.at[way, hop, piece], w_recv.at[way, hop, piece],
            along(way, core),
        )

    def across(hop, way, piece):
        here = quarter(hop, way, core, piece)
        return remote(
            here, here, core_send.at[way, hop, piece], core_recv.at[way, hop, piece],
            partner,
        )

    def head_send_copy(slot, way, owner):
        return remote(
            product.at[slot, pl.ds(way * HALF, HALF), :],
            gt_out.at[aligned(side, HALF), aligned(seq // 2, 2 * TOK)],
            g_send.at[slot, way], g_recv.at[seq], (owner, dp),
        )

    def head_local_copy(slot, way):
        return pltpu.make_async_copy(
            product.at[slot, pl.ds(way * HALF, HALF), :],
            gt_out.at[aligned(side, HALF), aligned(seq // 2, 2 * TOK)],
            g_local,
        )

    def owners(slot):
        if slot == 0:
            return z, (z + NZ // 2) % NZ
        return (z + NZ - slot) % NZ, (z + slot) % NZ

    def project(slot, ways):
        span = pl.ds(ways[0] * HALF, len(ways) * HALF)
        product[slot, span, :] = lax.dot_general(
            weights[slot, span, :], rows[...], (((1,), (1,)), ((), ())),
            preferred_element_type=jnp.float32,
        ).astype(jnp.bfloat16)
        for way in ways:
            owner = owners(slot)[way]

            @pl.when(owner != seq)
            def _(way=way, owner=owner):
                head_send_copy(slot, way, owner).start()

            @pl.when(owner == seq)
            def _(way=way):
                head_local_copy(slot, way).start()

    for hop in range(1, NZ // 2 + 1):
        ways = [way for way in (FWD, BWD) if hop <= HOPS[way]]
        for piece in range(PIECES):
            for way in ways:
                arrival(hop, way, piece).wait_recv()
                if hop < HOPS[way]:
                    onward(hop, way, piece).start()
                across(hop, way, piece).start()
        if hop == min(PROJECTS):
            row_here.wait()
            row_copy.wait_recv()

            @pl.when(core == side)
            def _():
                own_copy.wait()

            @pl.when(core != side)
            def _():
                remote(
                    w_in, weights.at[0, pl.ds(0, HALF), :], own_send, own_recv, partner
                ).wait_recv()

            project(0, (FWD,))
        for slot in PROJECTS.get(hop, ()):
            for piece in range(PIECES):
                for way in (FWD, BWD):
                    across(slot, way, piece).wait_recv()
            project(slot, (FWD, BWD))
    for piece in range(PIECES):
        across(NZ // 2, FWD, piece).wait_recv()
    project(0, (BWD,))

    @pl.when(core == side)
    def _():
        for copy in first_copies():
            copy.wait_send()

    for hop in range(1, NZ // 2 + 1):
        for piece in range(PIECES):
            for way in (FWD, BWD):
                if hop < HOPS[way]:
                    onward(hop, way, piece).wait_send()
                if hop <= HOPS[way]:
                    across(hop, way, piece).wait_send()
    row_copy.wait_send()
    for copy in head_here:
        copy.wait()
    for copy in head_copies:
        copy.wait()
    for slot in range(NZ // 2):
        for way, owner in enumerate(owners(slot)):
            @pl.when(owner != seq)
            def _(slot=slot, way=way, owner=owner):
                head_send_copy(slot, way, owner).wait_send()

            @pl.when(owner == seq)
            def _(slot=slot, way=way):
                head_local_copy(slot, way).wait()
    for other in range(NS):
        @pl.when(other != seq)
        def _(other=other):
            block = gt_out.at[pl.ds(0, HALF), pl.ds(0, 2 * TOK)]
            remote(
                block, block, g_send.at[0, 0], g_recv.at[other], (other, dp)
            ).wait_recv()


def gather_heads(q, k, v, g, w):
    dma = pltpu.SemaphoreType.DMA
    heads = jax.ShapeDtypeStruct((NS * TOK, HD), jnp.bfloat16)
    turned = jax.ShapeDtypeStruct((HD, NS * TOK), jnp.bfloat16)
    width = g.shape[1]
    anywhere = pl.BlockSpec(memory_space=pl.ANY)
    hops = NZ // 2 + 1
    return pl.pallas_call(
        gather_kernel,
        name="gather_heads",
        out_shape=[heads, heads, heads, turned],
        in_specs=[anywhere] * 5,
        out_specs=[anywhere] * 4,
        scratch_shapes=[
            pltpu.VMEM((2 * TOK, width), jnp.bfloat16),
            pltpu.VMEM((NZ // 2, HD, width), jnp.bfloat16),
            pltpu.VMEM((NZ // 2, HD, 2 * TOK), jnp.bfloat16),
            dma((3, len(OFFSETS))), dma((3, len(OFFSETS))), dma((3,)),
            dma, dma, dma,
            dma, dma((2, 2, PIECES)), dma, dma,
            dma((2, hops, PIECES)), dma((2, hops, PIECES)),
            dma((2, hops, PIECES)), dma((2, hops, PIECES)),
            dma((NZ // 2, 2)), dma((NS,)), dma,
        ],
        compiler_params=pltpu.CompilerParams(
            collective_id=0, has_side_effects=True, vmem_limit_bytes=GATHER_VMEM
        ),
    )(q, k, v, g, w)


def attention_kernel(
    lists, counts, q, k, v, gt, dq, dk, dv,
    pair_q, pair_k, k_turned, g_rows, score, prob_grad, top, total, delta,
    dq_sum, dk_sum, dv_sum,
):
    scale = HD ** -0.5
    exponent = scale * 1.4426950408889634

    used = jnp.int32(0)
    for i in range(NBLK):
        for j in range(KMAX):
            pair_q[used + j] = jnp.int32(i)
            pair_k[used + j] = lists[0, j, i]
        used = used + counts[0, i]
    for m in range(UNROLL):
        pair_q[used + m] = jnp.int32(0)
        pair_k[used + m] = jnp.int32(0)
    steps = (used + UNROLL - 1) // UNROLL

    dk_sum[...] = jnp.zeros_like(dk_sum)
    dv_sum[...] = jnp.zeros_like(dv_sum)
    dq_sum[...] = jnp.zeros_like(dq_sum)
    top[...] = jnp.full_like(top, -1e30)
    total[...] = jnp.zeros_like(total)
    delta[...] = jnp.zeros_like(delta)
    for t in range(NBLK):
        k_turned[t] = k[pl.ds(t * TOK, TOK), :].T
        g_rows[t] = gt[:, pl.ds(t * TOK, TOK)].T

    def tiles(x):
        return x.reshape(TOK // 8, 8, TOK)

    def each_pair(body):
        def step(n, carry):
            for m in range(UNROLL):
                t = n * UNROLL + m
                body(t, pair_q[t], pair_k[t])
            return carry

        lax.fori_loop(0, steps, step, 0)

    def scores(t, i, b):
        s = lax.dot_general(
            k[aligned(b, TOK), :], q[aligned(i, TOK), :], (((1,), (1,)), ((), ())),
            preferred_element_type=jnp.float32,
        )
        s = tiles(s) + jnp.where(t < used, 0.0, -1e30)
        score[t] = s
        top[i] = jnp.maximum(top[i], jnp.max(s, axis=0))
        prob_grad[t] = tiles(jnp.dot(
            v[aligned(b, TOK), :], gt[:, aligned(i, TOK)], preferred_element_type=jnp.float32
        ))

    each_pair(scores)
    top[...] = jnp.broadcast_to(
        jnp.max(top[...], axis=1, keepdims=True) * exponent, top.shape
    )

    def weigh(t, i, b):
        weight = jnp.exp2(score[t] * exponent - top[i])
        score[t] = weight
        total[i] += jnp.sum(weight, axis=0)
        delta[i] += jnp.sum(weight * prob_grad[t], axis=0)

    each_pair(weigh)
    inverse = 1.0 / jnp.sum(total[...], axis=1, keepdims=True)
    delta[...] = jnp.broadcast_to(
        jnp.sum(delta[...], axis=1, keepdims=True) * inverse, delta.shape
    )
    total[...] = jnp.broadcast_to(inverse, total.shape)

    def gradients(t, i, b):
        probs = score[t] * total[i]
        probs_low = probs.reshape(TOK, TOK).astype(jnp.bfloat16)
        score_low = (probs * (prob_grad[t] - delta[i])).reshape(TOK, TOK).astype(jnp.bfloat16)
        dv_sum[b] += jnp.dot(probs_low, g_rows[i], preferred_element_type=jnp.float32)
        dk_sum[b] += jnp.dot(
            score_low, q[aligned(i, TOK), :], preferred_element_type=jnp.float32
        )
        dq_sum[i] += jnp.dot(k_turned[b], score_low, preferred_element_type=jnp.float32)

    each_pair(gradients)
    for t in range(NBLK):
        rows = pl.ds(t * TOK, TOK)
        dq[rows, :] = (dq_sum[t].T * scale).astype(jnp.bfloat16)
        dk[rows, :] = (dk_sum[t] * scale).astype(jnp.bfloat16)
        dv[rows, :] = dv_sum[t].astype(jnp.bfloat16)


def attention_grads(lists, counts, q, k, v, gt):
    heads = jax.ShapeDtypeStruct((NBLK * TOK, HD), jnp.bfloat16)
    scalars = pl.BlockSpec(memory_space=pltpu.SMEM)
    whole = pl.BlockSpec(memory_space=pltpu.VMEM)
    blocks = (NBLK, TOK, HD)
    return pl.pallas_call(
        attention_kernel,
        name="attention_grads",
        out_shape=[heads] * 3,
        in_specs=[scalars] * 2 + [whole] * 4,
        out_specs=[whole] * 3,
        scratch_shapes=[
            pltpu.SMEM((PAIRS + KMAX + UNROLL,), jnp.int32),
            pltpu.SMEM((PAIRS + KMAX + UNROLL,), jnp.int32),
            pltpu.VMEM(blocks, jnp.bfloat16),
            pltpu.VMEM(blocks, jnp.bfloat16),
            pltpu.VMEM((PAIRS, TOK // 8, 8, TOK), jnp.float32),
            pltpu.VMEM((PAIRS, TOK // 8, 8, TOK), jnp.float32),
            pltpu.VMEM((NBLK, 8, TOK), jnp.float32),
            pltpu.VMEM((NBLK, 8, TOK), jnp.float32),
            pltpu.VMEM((NBLK, 8, TOK), jnp.float32),
            pltpu.VMEM(blocks, jnp.float32),
            pltpu.VMEM(blocks, jnp.float32),
            pltpu.VMEM(blocks, jnp.float32),
        ],
        compiler_params=pltpu.CompilerParams(vmem_limit_bytes=32 << 20),
    )(lists, counts, q, k, v, gt)


def scatter_kernel(*refs):
    ins, outs = refs[:3], refs[3:6]
    send_sem, recv_sem, local_sem = refs[6:]
    seq, dp = lax.axis_index("seq"), lax.axis_index("dp")
    peers = plane_peers(seq)
    enter([(p, dp) for p in peers])
    copies = []
    for n, (src, dst) in enumerate(zip(ins, outs)):
        for m, p in reversed(list(enumerate(peers))):
            copies.append(remote(
                src.at[aligned(p, TOK), :], dst.at[:, aligned(seq, HD)],
                send_sem.at[n, m], recv_sem.at[n, m], (p, dp),
            ))
            copies[-1].start()
    for n, (src, dst) in enumerate(zip(ins, outs)):
        copies.append(pltpu.make_async_copy(
            src.at[aligned(seq, TOK), :], dst.at[:, aligned(seq, HD)], local_sem.at[n]
        ))
        copies[-1].start()
    for copy in copies:
        copy.wait()


def scatter_heads(dq, dk, dv):
    dma = pltpu.SemaphoreType.DMA
    anywhere = pl.BlockSpec(memory_space=pl.ANY)
    return pl.pallas_call(
        scatter_kernel,
        name="scatter_heads",
        out_shape=[jax.ShapeDtypeStruct((TOK, NS * HD), jnp.bfloat16)] * 3,
        in_specs=[anywhere] * 3,
        out_specs=[anywhere] * 3,
        scratch_shapes=[dma((3, len(OFFSETS))), dma((3, len(OFFSETS))), dma((3,))],
        compiler_params=pltpu.CompilerParams(
            collective_id=1, has_side_effects=True, vmem_limit_bytes=24 << 20
        ),
    )(dq, dk, dv)


def store_kernel(*refs):
    copies = [
        pltpu.make_async_copy(src, dst, refs[6].at[n])
        for n, (src, dst) in enumerate(zip(refs[:3], refs[3:6]))
    ]
    for copy in copies:
        copy.start()
    for copy in copies:
        copy.wait()


def store_results(*arrays):
    anywhere = pl.BlockSpec(memory_space=pl.ANY)
    return pl.pallas_call(
        store_kernel,
        name="store_results",
        out_shape=[jax.ShapeDtypeStruct(a.shape, a.dtype) for a in arrays],
        in_specs=[anywhere] * 3,
        out_specs=[anywhere] * 3,
        scratch_shapes=[pltpu.SemaphoreType.DMA((3,))],
        compiler_params=pltpu.CompilerParams(vmem_limit_bytes=24 << 20),
    )(*arrays)


def local(queries, key_states, value_states, grad_out, out_weight, block_lists, block_counts):
    flat = [a.reshape(a.shape[1:]) for a in (queries, key_states, value_states, grad_out)]
    held = [pltpu.with_memory_space_constraint(a, pltpu.HBM) for a in (*flat, out_weight)]
    q, k, v, gt = gather_heads(*held)
    block_lists = pltpu.with_memory_space_constraint(jnp.swapaxes(block_lists, 1, 2), pltpu.HBM)
    block_counts = pltpu.with_memory_space_constraint(block_counts, pltpu.HBM)
    grads = attention_grads(block_lists, block_counts, q, k, v, gt)
    return tuple(out[None] for out in store_results(*scatter_heads(*grads)))


def solution(mesh):
    tokens = P("dp", "seq", None)
    return jax.shard_map(
        local,
        mesh=mesh,
        in_specs=(tokens,) * 4 + (P("dp", None), P("seq", None, None), P("seq", None)),
        out_specs=(tokens,) * 3,
        check_vma=False,
    )
```
